32 devices in a mesh: groups: 2 (over x), seq: 8 (over z, y), tp: 2 (over core).
Axes of the slice: x: 2, y: 2, z: 4, core: 2. Of those that a mesh axis runs over, the one named last changes fastest.
Arguments:
- queries: bfloat16 [4096, 8192], P(('groups', 'seq', 'tp')), parts along dimension 0, may hold values from -10 to 10
- keys: bfloat16 [4096, 1024], P(('groups', 'seq', 'tp')), parts along dimension 0, may hold values from -10 to 10
- values: bfloat16 [4096, 1024], P(('groups', 'seq', 'tp')), parts along dimension 0, may hold values from -6 to 6
- vertical_blocks: int32 [64, 2], replicated, may hold values from 0 to 15, as said below
- vertical_count: int32 [64], replicated, may hold values from 1 to 2, as said below
- slash_offsets: int32 [64, 2], replicated, may hold values from 1 to 15, as said below
- slash_count: int32 [64], replicated, may hold values from 1 to 2, as said below
Outputs:
- attention: bfloat16 [4096, 8192], P(('groups', 'seq', 'tp')), parts along dimension 0
The draws below stay inside these ranges and needn't reach their ends.
There are 2 independent parts, one for each index of `groups`. The reference program is written for one: setup_inputs(seed, part) draws one part's arguments, and reference() takes and returns one part's arrays. A program takes and returns all parts, laid end to end along the dimension named above; an argument that names none is the same for every part. Nothing has to cross between parts.
Inputs may be any that keep to these rules, and one draw needn't show every extreme that they name: `vertical_blocks`: the 2 entries of one head are distinct. `vertical_count`: some head uses all 2 entries. `slash_offsets`: the 2 entries of one head are distinct. `slash_count`: some head uses all 2 entries.
All inputs are finite; a program needn't handle non-finite values.
Results may differ from the reference program's by a relative error of at most 0.0037.
Values may be sent and summed in bfloat16 or wider, within the bound.
A program may use at most 128 MiB of HBM per device.

```python
import jax
import jax.numpy as jnp
from jax import lax

QUERY_HEADS = 64
KEY_VALUE_HEADS = 8
HEAD_SIZE = 128
MASK_BLOCK_SIZE = 128
NVMAX = 2
NSMAX = 2
SEQUENCE_LENGTH = 2048


def paired_draw(key):
    start_offset = jax.random.fold_in(key, 11)
    query_portion = jax.random.normal(jax.random.fold_in(start_offset, 1), (SEQUENCE_LENGTH, QUERY_HEADS, HEAD_SIZE), jnp.float32)
    key_portion = jax.random.normal(jax.random.fold_in(start_offset, 2), (SEQUENCE_LENGTH, KEY_VALUE_HEADS, HEAD_SIZE), jnp.float32)
    return (query_portion.reshape(SEQUENCE_LENGTH, QUERY_HEADS * HEAD_SIZE), key_portion.reshape(SEQUENCE_LENGTH, KEY_VALUE_HEADS * HEAD_SIZE))


def draw_queries(key, part):
    return paired_draw(key)[0].astype(jnp.bfloat16)


def draw_keys(key, part):
    return paired_draw(key)[1].astype(jnp.bfloat16)


def draw_vertical_blocks(key, part):
    head_keys = jax.random.split(jax.random.fold_in(key, 21), QUERY_HEADS)
    picked = jax.vmap(lambda one_key: jax.random.permutation(one_key, SEQUENCE_LENGTH // MASK_BLOCK_SIZE)[:NVMAX])(head_keys)
    return picked.astype(jnp.int32)


def draw_vertical_count(key, part):
    counts = jax.random.randint(jax.random.fold_in(key, 22), (QUERY_HEADS,), 1, NVMAX + 1)
    fullest = jax.random.randint(jax.random.fold_in(key, 23), (), 0, QUERY_HEADS)
    return counts.at[fullest].set(NVMAX).astype(jnp.int32)


def draw_slash_offsets(key, part):
    head_keys = jax.random.split(jax.random.fold_in(key, 31), QUERY_HEADS)
    picked = jax.vmap(lambda one_key: jax.random.permutation(one_key, SEQUENCE_LENGTH // MASK_BLOCK_SIZE - 1)[:NSMAX] + 1)(head_keys)
    return picked.astype(jnp.int32)


def draw_slash_count(key, part):
    counts = jax.random.randint(jax.random.fold_in(key, 32), (QUERY_HEADS,), 1, NSMAX + 1)
    fullest = jax.random.randint(jax.random.fold_in(key, 33), (), 0, QUERY_HEADS)
    return counts.at[fullest].set(NSMAX).astype(jnp.int32)


def steps_of(own_key, shape, cuts, low, top_value):
    def one(dim, parts):
        draws = jax.random.uniform(jax.random.fold_in(jax.random.fold_in(own_key, 6), dim), (parts,), jnp.float32, low / len(cuts), top_value / len(cuts))
        return jnp.repeat(jnp.exp(draws), shape[dim] // parts).reshape((-1,) + (1,) * (len(shape) - dim - 1))

    level = one(*cuts[0])
    for cut in cuts[1:]:
        level = level * one(*cut)
    return level


def gaussian(own_key, shape, spread, limit, cuts=(), held_as=jnp.bfloat16):
    gain = steps_of(own_key, shape, cuts, -0.22, 0.18) if cuts else 1.0
    values = jax.random.normal(own_key, shape, jnp.float32) * spread * gain
    return jnp.minimum(jnp.maximum(values, -limit), limit).astype(held_as)


def setup_inputs(seed: int = 0, part: int = 0) -> dict:
    seeds = jax.random.split(jax.random.key(seed), 8)
    part_splits = jax.random.split(jax.random.fold_in(seeds[7], part), 8)
    queries = draw_queries(jax.random.fold_in(jax.random.fold_in(seeds[7], part), 71), part)
    keys = draw_keys(jax.random.fold_in(jax.random.fold_in(seeds[7], part), 71), part)
    values = gaussian(part_splits[2], (SEQUENCE_LENGTH, KEY_VALUE_HEADS * HEAD_SIZE), 1.0, 6.0, ((0, 16),))
    vertical_blocks = draw_vertical_blocks(jax.random.fold_in(seeds[7], 71), part)
    vertical_count = draw_vertical_count(jax.random.fold_in(seeds[7], 71), part)
    slash_offsets = draw_slash_offsets(jax.random.fold_in(seeds[7], 71), part)
    slash_count = draw_slash_count(jax.random.fold_in(seeds[7], 71), part)
    return {"queries": queries, "keys": keys, "values": values, "vertical_blocks": vertical_blocks, "vertical_count": vertical_count, "slash_offsets": slash_offsets, "slash_count": slash_count}


def head_attend(query_blocks, block_index, row_offset, key_blocks, value_blocks, verticals, vertical_live, slash_list, slash_live):
    query_rows = query_blocks.shape[1]
    scaling = query_blocks.shape[2] ** -0.5
    total_block_count = key_blocks.shape[0]
    block_width = key_blocks.shape[1]
    block_total = block_index.shape[0]
    vertical_entries = jnp.arange(verticals.shape[0])
    slash_entries = jnp.arange(slash_list.shape[0])
    member = jnp.any((jnp.arange(total_block_count)[:, None] == verticals[None, :]) & (vertical_entries < vertical_live)[None, :], axis=1)
    vertical_active = (block_index[:, None] > verticals[None, :]) & (vertical_entries < vertical_live)[None, :]
    targets = block_index[:, None] - slash_list[None, :]
    safe_targets = jnp.clip(targets, 0, total_block_count - 1)
    slash_active = (targets >= 0) & (slash_entries < slash_live)[None, :] & jnp.logical_not(jnp.take(member, safe_targets))
    tile_index = jnp.concatenate([block_index[:, None],
                                  jnp.broadcast_to(verticals[None, :], (block_total, verticals.shape[0])),
                                  safe_targets], axis=1).astype(jnp.int32)
    tile_active = jnp.concatenate([jnp.ones((block_total, 1), bool), vertical_active, slash_active], axis=1)
    tile_keys = jnp.take(key_blocks, tile_index, axis=0).astype(jnp.float32)
    tile_values = jnp.take(value_blocks, tile_index, axis=0).astype(jnp.float32)
    scores = jnp.einsum("nqd,ntkd->nqtk", query_blocks.astype(jnp.float32), tile_keys) * scaling
    query_pos = row_offset + jnp.arange(query_rows)
    causal = query_pos[:, None] >= jnp.arange(block_width)[None, :]
    off_diagonal = (jnp.arange(tile_index.shape[1]) > 0)[None, None, :, None]
    allowed = tile_active[:, None, :, None] & (causal[None, :, None, :] | off_diagonal)
    scores = jnp.where(allowed, scores, -jnp.inf)
    peak = jnp.max(scores, axis=(2, 3))
    weights = jnp.exp(scores - peak[:, :, None, None])
    total = jnp.sum(weights, axis=(2, 3))
    rounded = lax.optimization_barrier(weights.astype(jnp.bfloat16)).astype(jnp.float32)
    numerator = jnp.einsum("nqtk,ntkd->nqd", rounded, tile_values)
    return (numerator / total[..., None]).astype(jnp.bfloat16)


def reference(queries, keys, values, vertical_blocks, vertical_count, slash_offsets, slash_count):
    total_block_count = SEQUENCE_LENGTH // MASK_BLOCK_SIZE
    heads_per_group = QUERY_HEADS // KEY_VALUE_HEADS
    query_heads = queries.reshape(total_block_count, MASK_BLOCK_SIZE, QUERY_HEADS, HEAD_SIZE)
    heads_of_keys = keys.reshape(total_block_count, MASK_BLOCK_SIZE, KEY_VALUE_HEADS, HEAD_SIZE)
    heads_of_values = values.reshape(total_block_count, MASK_BLOCK_SIZE, KEY_VALUE_HEADS, HEAD_SIZE)
    block_index = jnp.arange(total_block_count, dtype=jnp.int32)

    def one_head(head):
        query_blocks = lax.dynamic_index_in_dim(query_heads, head, 2, False)
        kv_head = head // heads_per_group
        key_blocks = lax.dynamic_index_in_dim(heads_of_keys, kv_head, 2, False)
        value_blocks = lax.dynamic_index_in_dim(heads_of_values, kv_head, 2, False)
        return head_attend(query_blocks, block_index, 0, key_blocks, value_blocks,
                           vertical_blocks[head], vertical_count[head], slash_offsets[head], slash_count[head])

    outputs = lax.map(one_head, jnp.arange(QUERY_HEADS, dtype=jnp.int32))
    return jnp.transpose(outputs, (1, 2, 0, 3)).reshape(SEQUENCE_LENGTH, QUERY_HEADS * HEAD_SIZE)
```

```python
import functools
import math

import jax
import jax.numpy as jnp
from jax import lax
from jax.experimental import pallas as pl
from jax.experimental.pallas import tpu as pltpu
from jax.sharding import PartitionSpec as P

HEAD_SIZE = 128
BLOCK = 128


def attend(q, block, head, load_key, load_value, vb, vc, so, sc, causal):
    nv, ns = vb.shape[1], so.shape[1]
    factor = HEAD_SIZE**-0.5 * math.log2(math.e)
    count_v, count_s = vc[head], sc[head]
    index, live = [block], []
    verticals = [vb[head, e] for e in range(nv)]
    for e in range(nv):
        index.append(verticals[e])
        live.append(jnp.logical_and(e < count_v, verticals[e] < block))
    for e in range(ns):
        target = block - so[head, e]
        ok = jnp.logical_and(e < count_s, target >= 0)
        for f in range(nv):
            taken = jnp.logical_and(f < count_v, verticals[f] == target)
            ok = jnp.logical_and(ok, jnp.logical_not(taken))
        index.append(jnp.maximum(target, 0))
        live.append(ok)
    keys = jnp.concatenate([load_key(t) for t in index], axis=0)
    scores = lax.dot_general(
        q, keys, (((1,), (1,)), ((), ())), preferred_element_type=jnp.float32
    )
    tiles = [jnp.where(causal, scores[:, :BLOCK], -jnp.inf)]
    for t, ok in enumerate(live):
        bias = jnp.where(ok, 0.0, -jnp.inf).astype(jnp.float32)
        tiles.append(scores[:, (t + 1) * BLOCK : (t + 2) * BLOCK] + bias)
    highest = functools.reduce(jnp.maximum, tiles)
    peak = jnp.max(highest, axis=1, keepdims=True) * factor
    weights = [jnp.exp2(t * factor - peak) for t in tiles]
    total = jnp.sum(functools.reduce(jnp.add, weights), axis=1, keepdims=True)
    rounded = jnp.concatenate([w.astype(jnp.bfloat16) for w in weights], axis=1)
    vals = jnp.concatenate([load_value(t) for t in index], axis=0)
    numerator = jnp.dot(rounded, vals, preferred_element_type=jnp.float32)
    return (numerator / total).astype(jnp.bfloat16)


def kernel(per_group, vb, vc, so, sc, q_ref, k_ref, v_ref, o_ref):
    rank = lax.axis_index("seq") * lax.axis_size("tp") + lax.axis_index("tp")
    group = pl.program_id(0)
    per_shard = q_ref.shape[0] // BLOCK
    rows = lax.broadcasted_iota(jnp.int32, (BLOCK, BLOCK), 0)
    causal = rows >= lax.broadcasted_iota(jnp.int32, (BLOCK, BLOCK), 1)
    for b in range(per_shard):
        span = slice(b * BLOCK, (b + 1) * BLOCK)
        for slot in range(per_group):
            cols = slice(slot * HEAD_SIZE, (slot + 1) * HEAD_SIZE)
            o_ref[span, cols] = attend(
                q_ref[span, cols],
                rank * per_shard + b,
                group * per_group + slot,
                lambda t: k_ref[pl.ds(pl.multiple_of(t * BLOCK, BLOCK), BLOCK), :],
                lambda t: v_ref[pl.ds(pl.multiple_of(t * BLOCK, BLOCK), BLOCK), :],
                vb, vc, so, sc, causal,
            )


def shards(queries, keys, values, vertical_blocks, vertical_count, slash_offsets, slash_count):
    heads = vertical_count.shape[0]
    groups = keys.shape[1] // HEAD_SIZE
    per_group = heads // groups
    tokens = queries.shape[0]
    all_keys = lax.all_gather(keys, ("seq", "tp"), axis=0, tiled=True)
    all_values = lax.all_gather(values, ("seq", "tp"), axis=0, tiled=True)
    smem = pl.BlockSpec(memory_space=pltpu.SMEM)
    length = all_keys.shape[0]
    return pl.pallas_call(
        functools.partial(kernel, per_group),
        grid=(groups,),
        in_specs=[smem] * 4
        + [
            pl.BlockSpec((tokens, per_group * HEAD_SIZE), lambda g: (0, g)),
            pl.BlockSpec((length, HEAD_SIZE), lambda g: (0, g)),
            pl.BlockSpec((length, HEAD_SIZE), lambda g: (0, g)),
        ],
        out_specs=pl.BlockSpec((tokens, per_group * HEAD_SIZE), lambda g: (0, g)),
        out_shape=jax.ShapeDtypeStruct(queries.shape, jnp.bfloat16),
        compiler_params=pltpu.CompilerParams(vmem_limit_bytes=48 * 1024 * 1024),
    )(vertical_blocks, vertical_count, slash_offsets, slash_count, queries, all_keys, all_values)


def solution(mesh):
    rows = P(("groups", "seq", "tp"), None)
    return jax.shard_map(
        shards,
        mesh=mesh,
        in_specs=(rows, rows, rows, P(), P(), P(), P()),
        out_specs=rows,
        check_vma=False,
    )
```

```python
import functools
import math

import jax
import jax.numpy as jnp
from jax import lax
from jax.experimental import pallas as pl
from jax.experimental.pallas import tpu as pltpu
from jax.sharding import PartitionSpec as P

HEAD_SIZE = 128
BLOCK = 128
SKEW = 2
PARTS = 2


def attend(q, block, head, load_key, load_value, vb, vc, so, sc, causal):
    nv, ns = vb.shape[1], so.shape[1]
    factor = HEAD_SIZE**-0.5 * math.log2(math.e)
    count_v, count_s = vc[head], sc[head]
    index, live = [block], []
    verticals = [vb[head, e] for e in range(nv)]
    for e in range(nv):
        index.append(verticals[e])
        live.append(jnp.logical_and(e < count_v, verticals[e] < block))
    for e in range(ns):
        target = block - so[head, e]
        ok = jnp.logical_and(e < count_s, target >= 0)
        for f in range(nv):
            taken = jnp.logical_and(f < count_v, verticals[f] == target)
            ok = jnp.logical_and(ok, jnp.logical_not(taken))
        index.append(jnp.maximum(target, 0))
        live.append(ok)
    keys = jnp.concatenate([load_key(t) for t in index], axis=0)
    scores = lax.dot_general(
        q, keys, (((1,), (1,)), ((), ())), preferred_element_type=jnp.float32
    )
    tiles = [jnp.where(causal, scores[:, :BLOCK], -jnp.inf)]
    for t, ok in enumerate(live):
        bias = jnp.where(ok, 0.0, -jnp.inf).astype(jnp.float32)
        tiles.append(scores[:, (t + 1) * BLOCK : (t + 2) * BLOCK] + bias)
    highest = functools.reduce(jnp.maximum, tiles)
    peak = jnp.max(highest, axis=1, keepdims=True) * factor
    weights = [jnp.exp2(t * factor - peak) for t in tiles]
    total = jnp.sum(functools.reduce(jnp.add, weights), axis=1, keepdims=True)
    rounded = jnp.concatenate([w.astype(jnp.bfloat16) for w in weights], axis=1)
    vals = jnp.concatenate([load_value(t) for t in index], axis=0)
    numerator = jnp.dot(rounded, vals, preferred_element_type=jnp.float32)
    return (numerator / total).astype(jnp.bfloat16)


def kernel(
    n, cores, per_group, slots, vb, vc, so, sc, q_hbm, k_hbm, v_hbm, o_hbm, *scratch
):
    kv = scratch[:slots]
    (q_buf, o_buf, loc_sem, sib_send, sib_recv, q_loc, q_send, q_recv,
     ring_send, ring_recv, o_loc, o_send, o_recv) = scratch[slots:]
    rank = lax.axis_index("seq")
    core = lax.axis_index("tp")
    other = 1 - core
    per_shard = q_hbm.shape[0] // BLOCK
    chip_blocks = cores * per_shard
    half = n // 2
    wide = per_group * HEAD_SIZE

    def at_position(p):
        p = lax.rem(p + n, n)
        late = p // half
        return (1 - late) * 2 * p + late * (2 * (n - 1 - p) + 1)

    odd = lax.rem(rank, 2)
    place = (1 - odd) * (rank // 2) + odd * (n - 1 - rank // 2)
    ahead, behind = at_position(place + 1), at_position(place - 1)

    barrier = pltpu.get_barrier_semaphore()
    for peer in ({"seq": ahead}, {"seq": behind}, {"tp": other}):
        pl.semaphore_signal(
            barrier, inc=1, device_id=peer, device_id_type=pl.DeviceIdType.MESH
        )

    def columns(owner, h, width):
        return pl.ds(pl.multiple_of((owner * slots + h) * width, width), width)

    def remote(src, dst, send, recv, peer):
        return pltpu.make_async_remote_copy(
            src_ref=src, dst_ref=dst, send_sem=send, recv_sem=recv,
            device_id=peer, device_id_type=pl.DeviceIdType.MESH,
        )

    def kv_local(h, which, b):
        source = (k_hbm, v_hbm)[which]
        spot = (rank * cores + core) * per_shard + b
        return pltpu.make_async_copy(
            source.at[pl.ds(b * BLOCK, BLOCK), columns(core, h, HEAD_SIZE)],
            kv[h].at[spot, which],
            loc_sem.at[h, which, b],
        )

    def kv_sibling(h, which, b, origin):
        source = (k_hbm, v_hbm)[which]
        spot = (rank * cores + origin) * per_shard + b
        return remote(
            source.at[pl.ds(b * BLOCK, BLOCK), columns(other, h, HEAD_SIZE)],
            kv[h].at[spot, which],
            sib_send.at[h, which, b], sib_recv.at[h, which, b], {"tp": other},
        )

    def q_local(h):
        return pltpu.make_async_copy(
            q_hbm.at[:, columns(core, h, wide)], q_buf.at[h, core], q_loc.at[h]
        )

    def q_sibling(h, origin):
        return remote(
            q_hbm.at[:, columns(other, h, wide)], q_buf.at[h, origin],
            q_send.at[h], q_recv.at[h], {"tp": other},
        )

    def hops(h, way):
        longer = half if h % 2 == way else n - 1 - half
        return longer

    def ring(h, way, j, incoming):
        step = 1 - 2 * way
        origin = place - step * (j if incoming else j - 1)
        chunk = kv[h].at[pl.ds(at_position(origin) * chip_blocks, chip_blocks)]
        peer = {"seq": (ahead, behind)[way]}
        return remote(
            chunk, chunk, ring_send.at[way, h, j - 1], ring_recv.at[way, h, j - 1], peer
        )

    pieces = [(which, b) for which in range(2) for b in range(per_shard)]
    for h in range(slots):
        for which, b in pieces:
            kv_local(h, which, b).start()
        q_local(h).start()
    pl.semaphore_wait(barrier, 3)
    for h in range(slots):
        for which, b in pieces:
            kv_sibling(h, which, b, core).start()
    for h in range(slots):
        q_sibling(h, core).start()

    def tick(t):
        for h in range(slots):
            j = t - SKEW * h
            if j == 1:
                for which, b in pieces:
                    kv_local(h, which, b).wait()
                    kv_sibling(h, which, b, other).wait_recv()
            for way in range(2):
                if 2 <= j <= hops(h, way) + 1:
                    ring(h, way, j - 1, True).wait_recv()
                if 1 <= j <= hops(h, way):
                    ring(h, way, j, False).start()

    rows = lax.broadcasted_iota(jnp.int32, (BLOCK, BLOCK), 0)
    causal = rows >= lax.broadcasted_iota(jnp.int32, (BLOCK, BLOCK), 1)
    share = per_group // PARTS
    narrow = share * HEAD_SIZE

    def compute(h, part):
        def one(slot):
            cols = pl.ds(pl.multiple_of(slot * HEAD_SIZE, HEAD_SIZE), HEAD_SIZE)
            for c in range(cores):
                for b in range(per_shard):
                    span = slice(b * BLOCK, (b + 1) * BLOCK)
                    o_buf[h, c, span, cols] = attend(
                        q_buf[h, c, span, cols],
                        (rank * cores + c) * per_shard + b,
                        (core * slots + h) * per_group + slot,
                        lambda t: kv[h][t, 0],
                        lambda t: kv[h][t, 1],
                        vb, vc, so, sc, causal,
                    )

        @pl.loop(part * share, (part + 1) * share)
        def _(slot):
            one(slot)

    def out_columns(h, part):
        start = (core * slots + h) * wide + part * narrow
        return pl.ds(pl.multiple_of(start, narrow), narrow)

    def out_local(h, part):
        return pltpu.make_async_copy(
            o_buf.at[h, core, :, pl.ds(part * narrow, narrow)],
            o_hbm.at[:, out_columns(h, part)],
            o_loc.at[h, part],
        )

    def out_sibling(h, part, incoming):
        owner = other if incoming else core
        start = (owner * slots + h) * wide + part * narrow
        return remote(
            o_buf.at[h, other, :, pl.ds(part * narrow, narrow)],
            o_hbm.at[:, pl.ds(pl.multiple_of(start, narrow), narrow)],
            o_send.at[h, part], o_recv.at[h, part], {"tp": other},
        )

    longest = half
    last_tick = SKEW * (slots - 1) + longest + 1
    done = 0
    pending = []
    for h in range(slots):
        while done < SKEW * h + longest + 1:
            done += 1
            tick(done)
        q_local(h).wait()
        q_sibling(h, other).wait_recv()
        for part in range(PARTS):
            compute(h, part)
            for item in pending:
                out_sibling(*item, False).start()
                out_local(*item).start()
            pending = [(h, part)]
            if done < min(last_tick, SKEW * (h + 1) + longest):
                done += 1
                tick(done)
    for item in pending:
        out_sibling(*item, False).start()
        out_local(*item).start()
    for h in range(slots):
        for which, b in pieces:
            kv_sibling(h, which, b, core).wait_send()
        q_sibling(h, core).wait_send()
        for way in range(2):
            for j in range(1, hops(h, way) + 1):
                ring(h, way, j, False).wait_send()
    for h in range(slots):
        for part in range(PARTS):
            out_local(h, part).wait()
            out_sibling(h, part, False).wait_send()
            out_sibling(h, part, True).wait_recv()


def shards(queries, keys, values, vertical_blocks, vertical_count, slash_offsets, slash_count):
    heads = vertical_count.shape[0]
    groups = keys.shape[1] // HEAD_SIZE
    per_group = heads // groups
    tokens = queries.shape[0]
    n, cores = lax.axis_size("seq"), lax.axis_size("tp")
    slots = groups // cores
    per_shard = tokens // BLOCK
    blocks = n * cores * per_shard
    smem = pl.BlockSpec(memory_space=pltpu.SMEM)
    hbm = pl.BlockSpec(memory_space=pl.ANY)
    dma = pltpu.SemaphoreType.DMA
    return pl.pallas_call(
        functools.partial(kernel, n, cores, per_group, slots),
        in_specs=[smem] * 4 + [hbm] * 3,
        out_specs=hbm,
        out_shape=jax.ShapeDtypeStruct(queries.shape, jnp.bfloat16),
        scratch_shapes=[pltpu.VMEM((blocks, 2, BLOCK, HEAD_SIZE), jnp.bfloat16)] * slots
        + [
            pltpu.VMEM((slots, cores, tokens, per_group * HEAD_SIZE), jnp.bfloat16),
            pltpu.VMEM((slots, cores, tokens, per_group * HEAD_SIZE), jnp.bfloat16),
            dma((slots, 2, per_shard)),
            dma((slots, 2, per_shard)),
            dma((slots, 2, per_shard)),
            dma((slots,)),
            dma((slots,)),
            dma((slots,)),
            dma((2, slots, n // 2)),
            dma((2, slots, n // 2)),
            dma((slots, PARTS)),
            dma((slots, PARTS)),
            dma((slots, PARTS)),
        ],
        compiler_params=pltpu.CompilerParams(
            collective_id=0, has_side_effects=True, vmem_limit_bytes=56 * 1024 * 1024
        ),
    )(vertical_blocks, vertical_count, slash_offsets, slash_count, queries, keys, values)


def solution(mesh):
    rows = P(("groups", "seq", "tp"), None)
    return jax.shard_map(
        shards,
        mesh=mesh,
        in_specs=(rows, rows, rows, P(), P(), P(), P()),
        out_specs=rows,
        check_vma=False,
    )
```

```python
import functools
import math

import jax
import jax.numpy as jnp
from jax import lax
from jax.experimental import pallas as pl
from jax.experimental.pallas import tpu as pltpu
from jax.sharding import PartitionSpec as P

HEAD_SIZE = 128
BLOCK = 128
SKEW = 3
PARTS = 4


def select(block, head, vb, vc, so, sc):
    nv, ns = vb.shape[0], so.shape[0]
    count_v, count_s = vc[head], sc[head]
    index, live = [block], []
    verticals = [vb[e, head] for e in range(nv)]
    for e in range(nv):
        index.append(verticals[e])
        live.append(jnp.logical_and(e < count_v, verticals[e] < block))
    for e in range(ns):
        target = block - so[e, head]
        ok = jnp.logical_and(e < count_s, target >= 0)
        for f in range(nv):
            taken = jnp.logical_and(f < count_v, verticals[f] == target)
            ok = jnp.logical_and(ok, jnp.logical_not(taken))
        index.append(jnp.maximum(target, 0))
        live.append(ok)
    return index, live


def score(q, keys, live, causal):
    scores = lax.dot_general(
        q, keys, (((1,), (1,)), ((), ())), preferred_element_type=jnp.float32
    )
    tiles = [jnp.where(causal, scores[:, :BLOCK], -jnp.inf)]
    for t, ok in enumerate(live):
        bias = jnp.where(ok, 0.0, -jnp.inf).astype(jnp.float32)
        tiles.append(scores[:, (t + 1) * BLOCK : (t + 2) * BLOCK] + bias)
    return tiles


def soften(tiles):
    factor = HEAD_SIZE**-0.5 * math.log2(math.e)
    highest = functools.reduce(jnp.maximum, tiles)
    peak = jnp.max(highest, axis=1, keepdims=True) * factor
    weights = [jnp.exp2(t * factor - peak) for t in tiles]
    total = jnp.sum(functools.reduce(jnp.add, weights), axis=1, keepdims=True)
    rounded = jnp.concatenate([w.astype(jnp.bfloat16) for w in weights], axis=1)
    return rounded, total


def kernel(
    n, cores, per_group, slots, vb, vc, so, sc, q_hbm, k_hbm, v_hbm, o_hbm, *scratch
):
    keys, values = scratch[:slots], scratch[slots : 2 * slots]
    (q_buf, o_buf, loc_sem, sib_send, sib_recv, q_loc, q_send, q_recv,
     ring_send, ring_recv, o_loc, o_send, o_recv) = scratch[2 * slots :]
    rank = lax.axis_index("seq")
    core = lax.axis_index("tp")
    other = 1 - core
    per_shard = q_hbm.shape[0] // BLOCK
    half = n // 2
    wide = per_group * HEAD_SIZE

    def at_position(p):
        p = lax.rem(p + n, n)
        late = p // half
        return (1 - late) * 2 * p + late * (2 * (n - 1 - p) + 1)

    odd = lax.rem(rank, 2)
    place = (1 - odd) * (rank // 2) + odd * (n - 1 - rank // 2)
    ahead, behind = at_position(place + 1), at_position(place - 1)

    barrier = pltpu.get_barrier_semaphore()
    for peer in ({"seq": ahead}, {"seq": behind}, {"tp": other}):
        pl.semaphore_signal(
            barrier, inc=1, device_id=peer, device_id_type=pl.DeviceIdType.MESH
        )

    def columns(owner, h, width):
        return pl.ds(pl.multiple_of((owner * slots + h) * width, width), width)

    def remote(src, dst, send, recv, peer):
        return pltpu.make_async_remote_copy(
            src_ref=src, dst_ref=dst, send_sem=send, recv_sem=recv,
            device_id=peer, device_id_type=pl.DeviceIdType.MESH,
        )

    def store(which, h):
        return (keys, values)[which][h]

    def kv_local(h, which, b):
        source = (k_hbm, v_hbm)[which]
        spot = (rank * cores + core) * per_shard + b
        return pltpu.make_async_copy(
            source.at[pl.ds(b * BLOCK, BLOCK), columns(core, h, HEAD_SIZE)],
            store(which, h).at[spot],
            loc_sem.at[h, which, b],
        )

    def kv_sibling(h, which, b, origin):
        source = (k_hbm, v_hbm)[which]
        spot = (rank * cores + origin) * per_shard + b
        return remote(
            source.at[pl.ds(b * BLOCK, BLOCK), columns(other, h, HEAD_SIZE)],
            store(which, h).at[spot],
            sib_send.at[h, which, b], sib_recv.at[h, which, b], {"tp": other},
        )

    def q_local(h):
        return pltpu.make_async_copy(
            q_hbm.at[:, columns(core, h, wide)], q_buf.at[h, core], q_loc.at[h]
        )

    def q_sibling(h, origin):
        return remote(
            q_hbm.at[:, columns(other, h, wide)], q_buf.at[h, origin],
            q_send.at[h], q_recv.at[h], {"tp": other},
        )

    def hops(h, way):
        return half if h % 2 == way else n - 1 - half

    def ring(h, way, j, piece, incoming):
        whose, which = piece
        step = 1 - 2 * way
        origin = place - step * (j if incoming else j - 1)
        spot = (at_position(origin) * cores + (core, other)[whose]) * per_shard
        chunk = store(which, h).at[pl.ds(spot, per_shard)]
        sem = (way, h, j - 1, 2 * whose + which)
        peer = {"seq": (ahead, behind)[way]}
        return remote(chunk, chunk, ring_send.at[sem], ring_recv.at[sem], peer)

    ring_pieces = [(whose, which) for whose in range(2) for which in range(2)]
    pieces = [(which, b) for which in range(2) for b in range(per_shard)]
    for h in range(slots):
        for which, b in pieces:
            kv_local(h, which, b).start()
    for h in range(slots):
        q_local(h).start()
    pl.semaphore_wait(barrier, 3)
    for h in range(slots):
        for which, b in pieces:
            kv_sibling(h, which, b, core).start()
    for h in range(slots):
        q_sibling(h, core).start()

    def event(h, way, j, piece):
        whose, which = piece
        if j == 1 and way == 0:
            for b in range(per_shard):
                if whose == 0:
                    kv_local(h, which, b).wait()
                else:
                    kv_sibling(h, which, b, other).wait_recv()
        if j >= 2:
            ring(h, way, j - 1, piece, True).wait_recv()
        if j <= hops(h, way):
            ring(h, way, j, piece, False).start()

    events, ready = [], []
    for t in range(1, SKEW * (slots - 1) + half + 2):
        for h in range(slots):
            j = t - SKEW * h
            for piece in ring_pieces:
                for way in range(2):
                    if 1 <= j <= hops(h, way) + 1:
                        events.append((h, way, j, piece))
            if j == half + 1:
                ready.append(len(events))

    rows = lax.broadcasted_iota(jnp.int32, (BLOCK, BLOCK), 0)
    causal = rows >= lax.broadcasted_iota(jnp.int32, (BLOCK, BLOCK), 1)

    def compute(h, slot, units):
        cols = slice(slot * HEAD_SIZE, (slot + 1) * HEAD_SIZE)
        head = (core * slots + h) * per_group + slot
        chosen = [
            select((rank * cores + c) * per_shard + b, head, vb, vc, so, sc)
            for c, b in units
        ]
        spans = [(c, slice(b * BLOCK, (b + 1) * BLOCK)) for c, b in units]
        tiles = [
            score(
                q_buf[h, c, span, cols],
                jnp.concatenate([keys[h][t] for t in index], axis=0),
                live,
                causal,
            )
            for (c, span), (index, live) in zip(spans, chosen)
        ]
        softened = [soften(t) for t in tiles]
        for (c, span), (index, _), (rounded, total) in zip(spans, chosen, softened):
            vals = jnp.concatenate([values[h][t] for t in index], axis=0)
            numerator = jnp.dot(rounded, vals, preferred_element_type=jnp.float32)
            o_buf[h, c, span, cols] = (numerator / total).astype(jnp.bfloat16)

    share = per_group // PARTS
    narrow = share * HEAD_SIZE

    def out_columns(owner, h, part):
        start = (owner * slots + h) * wide + part * narrow
        return pl.ds(pl.multiple_of(start, narrow), narrow)

    def out_local(h, part):
        return pltpu.make_async_copy(
            o_buf.at[h, core, :, pl.ds(part * narrow, narrow)],
            o_hbm.at[:, out_columns(core, h, part)],
            o_loc.at[h, part],
        )

    def out_sibling(h, part, incoming):
        return remote(
            o_buf.at[h, other, :, pl.ds(part * narrow, narrow)],
            o_hbm.at[:, out_columns(other if incoming else core, h, part)],
            o_send.at[h, part], o_recv.at[h, part], {"tp": other},
        )

    units = [(c, b) for c in range(cores) for b in range(per_shard)]
    done = 0
    pending = []
    for h in range(slots):
        while done < ready[h]:
            event(*events[done])
            done += 1
        q_local(h).wait()
        q_sibling(h, other).wait_recv()
        first = done
        rest = (ready[h + 1] if h + 1 < slots else len(events)) - first
        for slot in range(per_group):
            while done < first + rest * (slot + 1) // per_group:
                event(*events[done])
                done += 1
            compute(h, slot, units)
            if slot % share == share - 1:
                for item in pending:
                    out_sibling(*item, False).start()
                    out_local(*item).start()
                pending = [(h, slot // share)]
    for item in pending:
        out_sibling(*item, False).start()
        out_local(*item).start()
    for h in range(slots):
        for which, b in pieces:
            kv_sibling(h, which, b, core).wait_send()
        q_sibling(h, core).wait_send()
        for way in range(2):
            for j in range(1, hops(h, way) + 1):
                for piece in ring_pieces:
                    ring(h, way, j, piece, False).wait_send()
    for h in range(slots):
        for part in range(PARTS):
            out_local(h, part).wait()
            out_sibling(h, part, False).wait_send()
            out_sibling(h, part, True).wait_recv()


def shards(queries, keys, values, vertical_blocks, vertical_count, slash_offsets, slash_count):
    heads = vertical_count.shape[0]
    groups = keys.shape[1] // HEAD_SIZE
    per_group = heads // groups
    tokens = queries.shape[0]
    n, cores = lax.axis_size("seq"), lax.axis_size("tp")
    slots = groups // cores
    per_shard = tokens // BLOCK
    blocks = n * cores * per_shard
    smem = pl.BlockSpec(memory_space=pltpu.SMEM)
    hbm = pl.BlockSpec(memory_space=pl.ANY)
    dma = pltpu.SemaphoreType.DMA
    return pl.pallas_call(
        functools.partial(kernel, n, cores, per_group, slots),
        in_specs=[smem] * 4 + [hbm] * 3,
        out_specs=hbm,
        out_shape=jax.ShapeDtypeStruct(queries.shape, jnp.bfloat16),
        scratch_shapes=[pltpu.VMEM((blocks, BLOCK, HEAD_SIZE), jnp.bfloat16)] * (2 * slots)
        + [
            pltpu.VMEM((slots, cores, tokens, per_group * HEAD_SIZE), jnp.bfloat16),
            pltpu.VMEM((slots, cores, tokens, per_group * HEAD_SIZE), jnp.bfloat16),
            dma((slots, 2, per_shard)),
            dma((slots, 2, per_shard)),
            dma((slots, 2, per_shard)),
            dma((slots,)),
            dma((slots,)),
            dma((slots,)),
            dma((2, slots, n // 2, 4)),
            dma((2, slots, n // 2, 4)),
            dma((slots, PARTS)),
            dma((slots, PARTS)),
            dma((slots, PARTS)),
        ],
        compiler_params=pltpu.CompilerParams(
            collective_id=0, has_side_effects=True, vmem_limit_bytes=56 * 1024 * 1024
        ),
    )(vertical_blocks.T, vertical_count, slash_offsets.T, slash_count, queries, keys, values)


def solution(mesh):
    rows = P(("groups", "seq", "tp"), None)
    return jax.shard_map(
        shards,
        mesh=mesh,
        in_specs=(rows, rows, rows, P(), P(), P(), P()),
        out_specs=rows,
        check_vma=False,
    )
```

```python
import functools
import math

import jax
import jax.numpy as jnp
from jax import lax
from jax.experimental import pallas as pl
from jax.experimental.pallas import tpu as pltpu
from jax.sharding import PartitionSpec as P

HEAD_SIZE = 128
BLOCK = 128
SKEW = 1
PARTS = 4


def select(block, head, vb, vc, so, sc):
    nv, ns = vb.shape[0], so.shape[0]
    count_v, count_s = vc[head], sc[head]
    index, live = [block], []
    verticals = [vb[e, head] for e in range(nv)]
    for e in range(nv):
        index.append(verticals[e])
        live.append(jnp.logical_and(e < count_v, verticals[e] < block))
    for e in range(ns):
        target = block - so[e, head]
        ok = jnp.logical_and(e < count_s, target >= 0)
        for f in range(nv):
            taken = jnp.logical_and(f < count_v, verticals[f] == target)
            ok = jnp.logical_and(ok, jnp.logical_not(taken))
        index.append(jnp.maximum(target, 0))
        live.append(ok)
    return index, live


def score(q, keys, live, causal):
    scores = lax.dot_general(
        q, keys, (((1,), (1,)), ((), ())), preferred_element_type=jnp.float32
    )
    tiles = [jnp.where(causal, scores[:, :BLOCK], -jnp.inf)]
    for t, ok in enumerate(live):
        bias = jnp.where(ok, 0.0, -jnp.inf).astype(jnp.float32)
        tiles.append(scores[:, (t + 1) * BLOCK : (t + 2) * BLOCK] + bias)
    return tiles


def soften(tiles):
    factor = HEAD_SIZE**-0.5 * math.log2(math.e)
    highest = functools.reduce(jnp.maximum, tiles)
    peak = jnp.max(highest, axis=1, keepdims=True) * factor
    weights = [jnp.exp2(t * factor - peak) for t in tiles]
    total = jnp.sum(functools.reduce(jnp.add, weights), axis=1, keepdims=True)
    rounded = jnp.concatenate([w.astype(jnp.bfloat16) for w in weights], axis=1)
    return rounded, total


def kernel(
    n, cores, per_group, slots, vb, vc, so, sc, q_hbm, k_hbm, v_hbm, o_hbm, *scratch
):
    keys, values = scratch[:slots], scratch[slots : 2 * slots]
    (q_buf, o_buf, loc_sem, sib_send, sib_recv, q_loc, q_send, q_recv,
     ring_send, ring_recv, o_loc, o_send, o_recv) = scratch[2 * slots :]
    rank = lax.axis_index("seq")
    core = lax.axis_index("tp")
    other = 1 - core
    per_shard = q_hbm.shape[0] // BLOCK
    half = n // 2
    wide = per_group * HEAD_SIZE

    def at_position(p):
        p = lax.rem(p + n, n)
        late = p // half
        return (1 - late) * 2 * p + late * (2 * (n - 1 - p) + 1)

    odd = lax.rem(rank, 2)
    place = (1 - odd) * (rank // 2) + odd * (n - 1 - rank // 2)
    ahead, behind = at_position(place + 1), at_position(place - 1)

    barrier = pltpu.get_barrier_semaphore()
    for peer in ({"seq": ahead}, {"seq": behind}, {"tp": other}):
        pl.semaphore_signal(
            barrier, inc=1, device_id=peer, device_id_type=pl.DeviceIdType.MESH
        )

    def columns(owner, h, width):
        return pl.ds(pl.multiple_of((owner * slots + h) * width, width), width)

    def remote(src, dst, send, recv, peer):
        return pltpu.make_async_remote_copy(
            src_ref=src, dst_ref=dst, send_sem=send, recv_sem=recv,
            device_id=peer, device_id_type=pl.DeviceIdType.MESH,
        )

    def store(which, h):
        return (keys, values)[which][h]

    def kv_local(h, which, b):
        source = (k_hbm, v_hbm)[which]
        spot = (rank * cores + core) * per_shard + b
        return pltpu.make_async_copy(
            source.at[pl.ds(b * BLOCK, BLOCK), columns(core, h, HEAD_SIZE)],
            store(which, h).at[spot],
            loc_sem.at[h, which, b],
        )

    def kv_sibling(h, which, b, origin):
        source = (k_hbm, v_hbm)[which]
        spot = (rank * cores + origin) * per_shard + b
        return remote(
            source.at[pl.ds(b * BLOCK, BLOCK), columns(other, h, HEAD_SIZE)],
            store(which, h).at[spot],
            sib_send.at[h, which, b], sib_recv.at[h, which, b], {"tp": other},
        )

    def q_local(h):
        return pltpu.make_async_copy(
            q_hbm.at[:, columns(core, h, wide)], q_buf.at[h, core], q_loc.at[h]
        )

    def q_sibling(h, origin):
        return remote(
            q_hbm.at[:, columns(other, h, wide)], q_buf.at[h, origin],
            q_send.at[h], q_recv.at[h], {"tp": other},
        )

    def hops(h, way):
        return half if h % 2 == way else n - 1 - half

    def ring(h, way, j, piece, incoming):
        whose, which = piece
        step = 1 - 2 * way
        origin = place - step * (j if incoming else j - 1)
        spot = (at_position(origin) * cores + (core, other)[whose]) * per_shard
        chunk = store(which, h).at[pl.ds(spot, per_shard)]
        sem = (way, h, j - 1, 2 * whose + which)
        peer = {"seq": (ahead, behind)[way]}
        return remote(chunk, chunk, ring_send.at[sem], ring_recv.at[sem], peer)

    ring_pieces = [(whose, which) for whose in range(2) for which in range(2)]
    pieces = [(which, b) for which in range(2) for b in range(per_shard)]
    for h in range(slots):
        for which, b in pieces:
            kv_local(h, which, b).start()
    for h in range(slots):
        q_local(h).start()
    pl.semaphore_wait(barrier, 3)
    for h in range(slots):
        for which, b in pieces:
            kv_sibling(h, which, b, core).start()
    for h in range(slots):
        q_sibling(h, core).start()

    def event(h, way, j, piece):
        whose, which = piece
        if j == 1 and way == 0:
            for b in range(per_shard):
                if whose == 0:
                    kv_local(h, which, b).wait()
                else:
                    kv_sibling(h, which, b, other).wait_recv()
        if j >= 2:
            ring(h, way, j - 1, piece, True).wait_recv()
        if j <= hops(h, way):
            ring(h, way, j, piece, False).start()

    def start(h):
        return h * SKEW

    events, ready = [], []
    for t in range(1, start(slots - 1) + half + 2):
        for h in range(slots):
            j = t - start(h)
            for piece in ring_pieces:
                for way in range(2):
                    if 1 <= j <= hops(h, way) + 1:
                        events.append((h, way, j, piece))
            if j == half + 1:
                ready.append(len(events))

    rows = lax.broadcasted_iota(jnp.int32, (BLOCK, BLOCK), 0)
    causal = rows >= lax.broadcasted_iota(jnp.int32, (BLOCK, BLOCK), 1)

    def compute(h, slot, units):
        cols = slice(slot * HEAD_SIZE, (slot + 1) * HEAD_SIZE)
        head = (core * slots + h) * per_group + slot
        chosen = [
            select((rank * cores + c) * per_shard + b, head, vb, vc, so, sc)
            for c, b in units
        ]
        spans = [(c, slice(b * BLOCK, (b + 1) * BLOCK)) for c, b in units]
        tiles = [
            score(
                q_buf[h, c, span, cols],
                jnp.concatenate([keys[h][t] for t in index], axis=0),
                live,
                causal,
            )
            for (c, span), (index, live) in zip(spans, chosen)
        ]
        softened = [soften(t) for t in tiles]
        for (c, span), (index, _), (rounded, total) in zip(spans, chosen, softened):
            vals = jnp.concatenate([values[h][t] for t in index], axis=0)
            numerator = jnp.dot(rounded, vals, preferred_element_type=jnp.float32)
            o_buf[h, c, span, cols] = (numerator / total).astype(jnp.bfloat16)

    share = per_group // PARTS
    narrow = share * HEAD_SIZE

    def out_columns(owner, h, part):
        start = (owner * slots + h) * wide + part * narrow
        return pl.ds(pl.multiple_of(start, narrow), narrow)

    def out_local(h, part):
        return pltpu.make_async_copy(
            o_buf.at[h, core, :, pl.ds(part * narrow, narrow)],
            o_hbm.at[:, out_columns(core, h, part)],
            o_loc.at[h, part],
        )

    def out_sibling(h, part, incoming):
        return remote(
            o_buf.at[h, other, :, pl.ds(part * narrow, narrow)],
            o_hbm.at[:, out_columns(other if incoming else core, h, part)],
            o_send.at[h, part], o_recv.at[h, part], {"tp": other},
        )

    units = [(c, b) for c in range(cores) for b in range(per_shard)]
    done = 0
    pending = []
    for h in range(slots):
        while done < ready[h]:
            event(*events[done])
            done += 1
        q_local(h).wait()
        q_sibling(h, other).wait_recv()
        first = done
        rest = (ready[h + 1] if h + 1 < slots else len(events)) - first
        for slot in range(per_group):
            while done < first + rest * (slot + 1) // per_group:
                event(*events[done])
                done += 1
            compute(h, slot, units)
            if slot % share == share - 1:
                for item in pending:
                    out_sibling(*item, False).start()
                    out_local(*item).start()
                pending = [(h, slot // share)]
    for item in pending:
        out_sibling(*item, False).start()
        out_local(*item).start()
    for h in range(slots):
        for which, b in pieces:
            kv_sibling(h, which, b, core).wait_send()
        q_sibling(h, core).wait_send()
        for way in range(2):
            for j in range(1, hops(h, way) + 1):
                for piece in ring_pieces:
                    ring(h, way, j, piece, False).wait_send()
    for h in range(slots):
        for part in range(PARTS):
            out_local(h, part).wait()
            out_sibling(h, part, False).wait_send()
            out_sibling(h, part, True).wait_recv()


def shards(queries, keys, values, vertical_blocks, vertical_count, slash_offsets, slash_count):
    heads = vertical_count.shape[0]
    groups = keys.shape[1] // HEAD_SIZE
    per_group = heads // groups
    tokens = queries.shape[0]
    n, cores = lax.axis_size("seq"), lax.axis_size("tp")
    slots = groups // cores
    per_shard = tokens // BLOCK
    blocks = n * cores * per_shard
    smem = pl.BlockSpec(memory_space=pltpu.SMEM)
    hbm = pl.BlockSpec(memory_space=pl.ANY)
    dma = pltpu.SemaphoreType.DMA
    return pl.pallas_call(
        functools.partial(kernel, n, cores, per_group, slots),
        in_specs=[smem] * 4 + [hbm] * 3,
        out_specs=hbm,
        out_shape=jax.ShapeDtypeStruct(queries.shape, jnp.bfloat16),
        scratch_shapes=[pltpu.VMEM((blocks, BLOCK, HEAD_SIZE), jnp.bfloat16)] * (2 * slots)
        + [
            pltpu.VMEM((slots, cores, tokens, per_group * HEAD_SIZE), jnp.bfloat16),
            pltpu.VMEM((slots, cores, tokens, per_group * HEAD_SIZE), jnp.bfloat16),
            dma((slots, 2, per_shard)),
            dma((slots, 2, per_shard)),
            dma((slots, 2, per_shard)),
            dma((slots,)),
            dma((slots,)),
            dma((slots,)),
            dma((2, slots, n // 2, 4)),
            dma((2, slots, n // 2, 4)),
            dma((slots, PARTS)),
            dma((slots, PARTS)),
            dma((slots, PARTS)),
        ],
        compiler_params=pltpu.CompilerParams(
            collective_id=0, has_side_effects=True, vmem_limit_bytes=56 * 1024 * 1024
        ),
    )(vertical_blocks.T, vertical_count, slash_offsets.T, slash_count, queries, keys, values)


def solution(mesh):
    rows = P(("groups", "seq", "tp"), None)
    return jax.shard_map(
        shards,
        mesh=mesh,
        in_specs=(rows, rows, rows, P(), P(), P(), P()),
        out_specs=rows,
        check_vma=False,
    )
```
